32 devices in a mesh: head: 8 (over z, x), seq: 4 (over y, core).
Axes of the slice: x: 2, y: 2, z: 4, core: 2. Of those that a mesh axis runs over, the one named last changes fastest.
Arguments:
- queries: bfloat16 [4, 1024, 4096], P('seq', 'head'), may hold values from -8 to 8
- key_row_matrix: bfloat16 [4, 1024, 1024], P('seq', 'head'), may hold values from -8 to 8
- values: bfloat16 [4, 1024, 1024], P('seq', 'head'), may hold values from -6 to 6
- verticals: int32 [32, 6], replicated, may hold values from 0 to 31, as said below
- slashes: int32 [32, 3], replicated, may hold values from 1 to 7, as said below
- counts: int32 [32, 2], replicated, may hold values from 0 to 6, as said below
Outputs:
- context: bfloat16 [4, 1024, 4096], P('seq', 'head')
The draws below stay inside these ranges and needn't reach their ends.
Inputs may be any that keep to these rules, and one draw needn't show every extreme that they name: `verticals`: each row holds 6 different key blocks. `slashes`: each row holds 3 different block offsets. `counts`: column 0 is at least 1; some head uses all 6 and all 3 slots.
All inputs are finite; a program needn't handle non-finite values.
Results may differ from the reference program's by a relative error of at most 0.0037.
Values may be sent and summed in bfloat16 or wider, within the bound.
A program may use at most 64 MiB of HBM per device.

```python
import math
import jax
import jax.numpy as jnp
from jax import lax

QUERY_HEADS = 32
KEY_VALUE_HEADS = 8
HEAD_WIDTH = 128
BLOCK_TOKENS = 128
NV = 6
NS = 3
SEGMENT_TOKENS = 1024
SEGBLK = 8
SEGMENT_COUNT = 4
BLOCK_COUNT = 32


def draw_queries(key, part):
    array_shape = (SEGMENT_COUNT, SEGMENT_TOKENS, QUERY_HEADS * HEAD_WIDTH)
    drawn = jax.random.truncated_normal(jax.random.fold_in(key, 11), -6.0, 6.0, array_shape)
    return drawn.astype(jnp.bfloat16)


def draw_key_row_matrix(key, part):
    array_shape = (SEGMENT_COUNT, SEGMENT_TOKENS, KEY_VALUE_HEADS * HEAD_WIDTH)
    drawn = jax.random.truncated_normal(jax.random.fold_in(key, 13), -6.0, 6.0, array_shape)
    return drawn.astype(jnp.bfloat16)


def draw_verticals(key, part):
    head_keys = jax.random.split(jax.random.fold_in(key, 21), QUERY_HEADS)
    picked = jax.vmap(lambda item: jax.random.permutation(item, BLOCK_COUNT)[:NV])(head_keys)
    return picked.astype(jnp.int32)


def draw_slashes(key, part):
    head_keys = jax.random.split(jax.random.fold_in(key, 31), QUERY_HEADS)
    picked = jax.vmap(lambda item: jax.random.permutation(item, SEGBLK - 1)[:NS] + 1)(head_keys)
    widest = jnp.concatenate([jax.random.permutation(jax.random.fold_in(key, 32), SEGBLK - 2)[:NS - 1] + 1, jnp.array([SEGBLK - 1], dtype=jnp.int32)])
    chosen = jax.random.randint(jax.random.fold_in(key, 33), (), 0, QUERY_HEADS)
    picked = picked.at[chosen].set(widest.astype(picked.dtype))
    return picked.astype(jnp.int32)


def draw_counts(key, part):
    dense = jax.random.randint(jax.random.fold_in(key, 41), (QUERY_HEADS,), 0, 4) == 0
    light_columns = jax.random.randint(jax.random.fold_in(key, 42), (QUERY_HEADS,), 1, 3)
    light_slashes = jax.random.randint(jax.random.fold_in(key, 43), (QUERY_HEADS,), 0, 2)
    fullest = jax.random.randint(jax.random.fold_in(key, 44), (), 0, QUERY_HEADS)
    sparsest = (fullest + jax.random.randint(jax.random.fold_in(key, 45), (), 1, QUERY_HEADS)) % QUERY_HEADS
    column_use = jnp.where(dense, NV, light_columns)
    slash_use = jnp.where(dense, NS, light_slashes)
    column_use = column_use.at[fullest].set(NV).at[sparsest].set(1)
    slash_use = slash_use.at[fullest].set(NS).at[sparsest].set(0)
    return jnp.stack([column_use, slash_use], axis=1).astype(jnp.int32)


def level_of(stream_key, dims, cuts, smallest, largest):
    gain, own = 1.0, jax.random.fold_in(stream_key, 6)
    for axis_at, shards_of in cuts:
        heights = jnp.exp(jax.random.uniform(jax.random.fold_in(own, axis_at), (shards_of,), jnp.float32, smallest / len(cuts), largest / len(cuts)))
        gain = gain * jnp.repeat(heights, dims[axis_at] // shards_of).reshape([-1 if axis == axis_at else 1 for axis in range(len(dims))])
    return gain


def scatter_about(stream_key, dims, width, bound, cuts=(), held_as=jnp.bfloat16):
    result = width * jax.random.normal(stream_key, dims, jnp.float32)
    if cuts:
        result = result * level_of(stream_key, dims, cuts, -0.22, 0.18)
    return jnp.clip(result, -bound, bound).astype(held_as)


def setup_inputs(seed: int = 0) -> dict:
    seeds = jax.random.split(jax.random.key(seed), 7)
    return {
        "queries": draw_queries(jax.random.fold_in(seeds[6], 71), 0),
        "key_row_matrix": draw_key_row_matrix(jax.random.fold_in(seeds[6], 71), 0),
        "values": scatter_about(seeds[2], (SEGMENT_COUNT, SEGMENT_TOKENS, KEY_VALUE_HEADS * HEAD_WIDTH), 1.0, 6.0, ((0, 4), (1, 8))),
        "verticals": draw_verticals(jax.random.fold_in(seeds[6], 71), 0),
        "slashes": draw_slashes(jax.random.fold_in(seeds[6], 71), 0),
        "counts": draw_counts(jax.random.fold_in(seeds[6], 71), 0),
    }


def head_attention(query, key_block, value_block, columns, offsets, in_use):
    group_ids = jnp.arange(SEGBLK, dtype=jnp.int32)
    row_ids = jnp.arange(BLOCK_TOKENS, dtype=jnp.int32)
    causal = row_ids[:, None] >= row_ids[None, :]
    slash_live = jnp.arange(NS, dtype=jnp.int32) < in_use[1]
    column_live = jnp.arange(NV, dtype=jnp.int32) < in_use[0]
    later_slot = jnp.arange(1 + NS + NV, dtype=jnp.int32) > 0
    scaling = 1.0 / math.sqrt(HEAD_WIDTH)

    def segment(seg_id):
        block_ids = seg_id * SEGBLK + group_ids
        slash_ids = block_ids[:, None] - offsets[None, :]
        slash_ok = slash_live[None, :] & (slash_ids >= 0)
        repeated = jnp.any(slash_live[None, None, :] & (block_ids[:, None, None] - columns[None, :, None] == offsets[None, None, :]), axis=2)
        column_ok = column_live[None, :] & (columns[None, :] < block_ids[:, None]) & jnp.logical_not(repeated)
        column_ids = jnp.broadcast_to(columns[None, :], (SEGBLK, NV))
        chosen = jnp.concatenate([block_ids[:, None], slash_ids, column_ids], axis=1)
        allowed = jnp.concatenate([jnp.ones((SEGBLK, 1), dtype=bool), slash_ok, column_ok], axis=1)
        chosen = jnp.clip(chosen, 0, BLOCK_COUNT - 1).astype(jnp.int32)
        key_take = key_block[chosen].astype(jnp.float32)
        value_take = value_block[chosen].astype(jnp.float32)
        query_here = lax.dynamic_slice_in_dim(query, seg_id * SEGBLK, SEGBLK, 0).astype(jnp.float32)
        scores = jnp.einsum('gqd,gskd->gqsk', query_here, key_take) * scaling
        visible = allowed[:, None, :, None] & (later_slot[None, None, :, None] | causal[None, :, None, :])
        scores = jnp.where(visible, scores, -jnp.inf)
        row_top = lax.optimization_barrier(jnp.max(scores, axis=(2, 3), keepdims=True))
        weights = jnp.exp(scores - row_top)
        totals = lax.optimization_barrier(jnp.sum(weights, axis=(2, 3)))
        rounded = lax.optimization_barrier(weights.astype(jnp.bfloat16)).astype(jnp.float32)
        mixed = jnp.einsum('gqsk,gskd->gqd', rounded, value_take)
        return (mixed / totals[:, :, None]).astype(jnp.bfloat16)
    return lax.map(segment, jnp.arange(SEGMENT_COUNT, dtype=jnp.int32))

def reference(queries, key_row_matrix, values, verticals, slashes, counts):
    query_all = queries.reshape(BLOCK_COUNT, BLOCK_TOKENS, QUERY_HEADS, HEAD_WIDTH)
    key_complete = key_row_matrix.reshape(BLOCK_COUNT, BLOCK_TOKENS, KEY_VALUE_HEADS, HEAD_WIDTH)
    value_complete = values.reshape(BLOCK_COUNT, BLOCK_TOKENS, KEY_VALUE_HEADS, HEAD_WIDTH)
    group_width = QUERY_HEADS // KEY_VALUE_HEADS

    def one_head(head_id):
        shared = head_id // group_width
        query = lax.dynamic_index_in_dim(query_all, head_id, 2, keepdims=False)
        key_block = lax.dynamic_index_in_dim(key_complete, shared, 2, keepdims=False)
        value_block = lax.dynamic_index_in_dim(value_complete, shared, 2, keepdims=False)
        return head_attention(query, key_block, value_block, verticals[head_id], slashes[head_id], counts[head_id])
    outputs = lax.map(one_head, jnp.arange(QUERY_HEADS, dtype=jnp.int32))
    outputs = jnp.transpose(outputs, (1, 2, 3, 0, 4))
    return outputs.reshape(SEGMENT_COUNT, SEGMENT_TOKENS, QUERY_HEADS * HEAD_WIDTH)
```

```python
import functools
import math

import jax
import jax.numpy as jnp
from jax import lax
from jax.experimental import pallas as pl
from jax.experimental.pallas import tpu as pltpu
from jax.sharding import PartitionSpec as P

QUERY_HEADS = 32
KEY_VALUE_HEADS = 8
HEAD_WIDTH = 128
BLOCK_TOKENS = 128
GROUP = KEY_VALUE_HEADS
SHARED = QUERY_HEADS // KEY_VALUE_HEADS
WIDE = SHARED * HEAD_WIDTH
ORDER = (4, 2, 6, 5, 3, 7, 1)
MESH = pl.DeviceIdType.MESH
VMEM = pl.BlockSpec(memory_space=pltpu.VMEM)
SMEM = pl.BlockSpec(memory_space=pltpu.SMEM)


def flipped(member, bits):
    parts = (member % 2, (member // 2) % 2, member // 4)
    return sum(((part + ((bits >> k) & 1)) % 2) * (1 << k) for k, part in enumerate(parts))


def place():
    seqs = lax.axis_size("seq")
    number = lax.axis_index("head") * seqs + lax.axis_index("seq")
    return seqs, number, number // GROUP, number % GROUP


def greet(barrier, seqs, number):
    pl.semaphore_signal(
        barrier, inc=1, device_id=(number // seqs, number % seqs), device_id_type=MESH
    )


def spread_kernel(
    groups, q_in, k_in, v_in, q_out, kv_out, own, kv_send, kv_got, q_send, q_got, z_send, z_got
):
    seqs, me, plane, member = place()
    base = plane * GROUP
    has_above = plane < groups - 1
    has_below = plane > 0
    barrier = pltpu.get_barrier_semaphore()
    for bits in ORDER:
        greet(barrier, seqs, base + flipped(member, bits))

    @pl.when(has_above)
    def _():
        greet(barrier, seqs, me + GROUP)

    @pl.when(has_below)
    def _():
        greet(barrier, seqs, me - GROUP)

    def narrow(ref, to):
        return ref.at[:, pl.ds(pl.multiple_of(to * HEAD_WIDTH, HEAD_WIDTH), HEAD_WIDTH)]

    def wide(ref, to):
        return ref.at[:, pl.ds(pl.multiple_of(to * WIDE, WIDE), WIDE)]

    stay = [
        pltpu.make_async_copy(narrow(k_in, member), kv_out.at[me, 0], own.at[0]),
        pltpu.make_async_copy(narrow(v_in, member), kv_out.at[me, 1], own.at[1]),
        pltpu.make_async_copy(wide(q_in, member), q_out.at[member], own.at[2]),
    ]
    for copy in stay:
        copy.start()
    pl.semaphore_wait(
        barrier, GROUP - 1 + jnp.where(has_above, 1, 0) + jnp.where(has_below, 1, 0)
    )

    def remote(src, dst, send, got, to):
        return pltpu.make_async_remote_copy(
            src_ref=src,
            dst_ref=dst,
            send_sem=send,
            recv_sem=got,
            device_id=(to // seqs, to % seqs),
            device_id_type=MESH,
        )

    kv_copies, q_copies = [], []
    for bits in ORDER:
        to = flipped(member, bits)
        for which, ref in enumerate((k_in, v_in)):
            kv_copies.append(
                remote(
                    narrow(ref, to),
                    kv_out.at[me, which],
                    kv_send.at[which, bits],
                    kv_got.at[which, bits],
                    base + to,
                )
            )
            kv_copies[-1].start()
    for bits in ORDER:
        to = flipped(member, bits)
        q_copies.append(
            remote(wide(q_in, to), q_out.at[member], q_send.at[bits], q_got.at[bits], base + to)
        )
        q_copies[-1].start()

    def up(block):
        return remote(
            kv_out.at[block], kv_out.at[block], z_send.at[0, block], z_got.at[block], me + GROUP
        )

    def down(block):
        return remote(
            kv_out.at[block], kv_out.at[block], z_send.at[1, block], z_got.at[block], me - GROUP
        )

    def pass_on(block, upward, downward):
        if upward:

            @pl.when(has_above)
            def _():
                up(block).start()

        if downward:

            @pl.when(has_below)
            def _():
                down(block).start()

    stay[0].wait()
    stay[1].wait()
    pass_on(me, True, True)
    for at, bits in enumerate(ORDER):
        kv_copies[2 * at].wait_recv()
        kv_copies[2 * at + 1].wait_recv()
        pass_on(base + flipped(member, bits), True, True)

    def far_step(step, carry):
        for bits in (0,) + ORDER:
            other = flipped(member, bits)
            lower = (plane - step) * GROUP + other
            upper = (plane + step) * GROUP + other

            @pl.when(plane - step >= 0)
            def _():
                up(lower).wait_recv()
                pass_on(lower, True, False)

            @pl.when(plane + step < groups)
            def _():
                down(upper).wait_recv()
                pass_on(upper, False, True)

        return carry

    lax.fori_loop(1, groups, far_step, 0)
    stay[2].wait()
    for copy in kv_copies:
        copy.wait_send()
    for copy in q_copies:
        copy.wait()

    def sent_step(step, carry):
        for other in range(GROUP):
            block = step * GROUP + other

            @pl.when(has_above & (step <= plane))
            def _():
                up(block).wait_send()

            @pl.when(has_below & (step >= plane))
            def _():
                down(block).wait_send()

        return carry

    lax.fori_loop(0, groups, sent_step, 0)


def spread(queries, keys, values, groups):
    count = groups * GROUP
    rows = queries.shape[0]
    return pl.pallas_call(
        functools.partial(spread_kernel, groups),
        name="spread",
        out_shape=(
            jax.ShapeDtypeStruct((GROUP, rows, WIDE), jnp.bfloat16),
            jax.ShapeDtypeStruct((count, 2, rows, HEAD_WIDTH), jnp.bfloat16),
        ),
        in_specs=[VMEM] * 3,
        out_specs=(VMEM, VMEM),
        scratch_shapes=[
            pltpu.SemaphoreType.DMA((3,)),
            pltpu.SemaphoreType.DMA((2, GROUP)),
            pltpu.SemaphoreType.DMA((2, GROUP)),
            pltpu.SemaphoreType.DMA((GROUP,)),
            pltpu.SemaphoreType.DMA((GROUP,)),
            pltpu.SemaphoreType.DMA((2, count)),
            pltpu.SemaphoreType.DMA((count,)),
        ],
        compiler_params=pltpu.CompilerParams(collective_id=0, has_side_effects=True),
    )(queries, keys, values)


def attend_kernel(verticals, slashes, counts, q, kv, out, scores, top, total, mixed):
    heads = lax.axis_size("head")
    seqs, me, plane, member = place()
    base = plane * GROUP
    slash_slots = slashes.shape[1]
    factor = math.log2(math.e) / math.sqrt(HEAD_WIDTH)
    rows = lax.broadcasted_iota(jnp.int32, (BLOCK_TOKENS, BLOCK_TOKENS), 0)
    cols = lax.broadcasted_iota(jnp.int32, (BLOCK_TOKENS, BLOCK_TOKENS), 1)
    causal = rows >= cols
    block_ids = [
        ((base + t) % seqs) * heads + (base + t) // seqs for t in range(GROUP)
    ]

    def holder(block):
        return (block % heads) * seqs + block // heads

    def product(left, right, dims):
        return lax.dot_general(left, right, (dims, ((), ())), preferred_element_type=jnp.float32)

    def one_head(j, carry):
        head = member * SHARED + j
        columns = pl.ds(pl.multiple_of(j * HEAD_WIDTH, HEAD_WIDTH), HEAD_WIDTH)
        n_slash = counts[head, 1]
        n_column = counts[head, 0]

        def keep(slot, t, key, active):
            found = product(q[t, :, columns], key, ((1,), (1,)))
            found = jnp.where(active, found, -jnp.inf)
            scores[slot, t] = found
            top[t] = jnp.maximum(top[t], found)

        for t in range(GROUP):
            found = product(q[t, :, columns], kv[base + t, 0], ((1,), (1,)))
            found = jnp.where(causal, found, -jnp.inf)
            scores[0, t] = found
            top[t] = found

        def slash_scores(slot, carry):
            offset = slashes[head, slot]
            for t in range(GROUP):
                block = block_ids[t] - offset
                keep(1 + slot, t, kv[holder(jnp.maximum(block, 0)), 0], block >= 0)
            return carry

        def column_scores(slot, carry):
            column = verticals[head, slot]
            key = kv[holder(column), 0]
            for t in range(GROUP):
                active = column < block_ids[t]
                for s in range(slash_slots):
                    repeated = (block_ids[t] - column == slashes[head, s]) & (s < n_slash)
                    active = active & jnp.logical_not(repeated)
                keep(1 + n_slash + slot, t, key, active)
            return carry

        lax.fori_loop(0, n_slash, slash_scores, 0)
        lax.fori_loop(0, n_column, column_scores, 0)

        def weigh(slot, t, first, value):
            weights = jnp.exp2((scores[slot, t] - top[t]) * factor)
            part = product(weights.astype(jnp.bfloat16), value, ((1,), (0,)))
            if first:
                total[t] = weights
                mixed[t] = part
            else:
                total[t] = total[t] + weights
                mixed[t] = mixed[t] + part

        for t in range(GROUP):
            top[t] = jnp.broadcast_to(jnp.max(top[t], axis=1, keepdims=True), top.shape[1:])
        for t in range(GROUP):
            weigh(0, t, True, kv[base + t, 1])

        def slash_mix(slot, carry):
            offset = slashes[head, slot]
            for t in range(GROUP):
                block = jnp.maximum(block_ids[t] - offset, 0)
                weigh(1 + slot, t, False, kv[holder(block), 1])
            return carry

        def column_mix(slot, carry):
            value = kv[holder(verticals[head, slot]), 1]
            for t in range(GROUP):
                weigh(1 + n_slash + slot, t, False, value)
            return carry

        lax.fori_loop(0, n_slash, slash_mix, 0)
        lax.fori_loop(0, n_column, column_mix, 0)
        for t in range(GROUP):
            sums = jnp.sum(total[t], axis=1, keepdims=True)
            out[t, :, columns] = (mixed[t] / sums).astype(out.dtype)
        return carry

    lax.fori_loop(0, SHARED, one_head, 0)


def attend(verticals, slashes, counts, queries, pairs):
    slots = 1 + verticals.shape[1] + slashes.shape[1]
    tile = (BLOCK_TOKENS, BLOCK_TOKENS)
    return pl.pallas_call(
        attend_kernel,
        name="attend",
        out_shape=jax.ShapeDtypeStruct(queries.shape, jnp.bfloat16),
        in_specs=[SMEM] * 3 + [VMEM] * 2,
        out_specs=VMEM,
        scratch_shapes=[
            pltpu.VMEM((slots, GROUP) + tile, jnp.float32),
            pltpu.VMEM((GROUP,) + tile, jnp.float32),
            pltpu.VMEM((GROUP,) + tile, jnp.float32),
            pltpu.VMEM((GROUP,) + tile, jnp.float32),
        ],
    )(verticals, slashes, counts, queries, pairs)


def collect_kernel(o_in, out, own, send, got):
    seqs, me, plane, member = place()
    base = plane * GROUP
    barrier = pltpu.get_barrier_semaphore()
    for bits in ORDER:
        greet(barrier, seqs, base + flipped(member, bits))
    mine = out.at[:, pl.ds(pl.multiple_of(member * WIDE, WIDE), WIDE)]
    stay = pltpu.make_async_copy(o_in.at[member], mine, own)
    stay.start()
    pl.semaphore_wait(barrier, GROUP - 1)
    copies = []
    for bits in ORDER:
        to = flipped(member, bits)
        copies.append(
            pltpu.make_async_remote_copy(
                src_ref=o_in.at[to],
                dst_ref=mine,
                send_sem=send.at[bits],
                recv_sem=got.at[bits],
                device_id=((base + to) // seqs, (base + to) % seqs),
                device_id_type=MESH,
            )
        )
        copies[-1].start()
    stay.wait()
    for copy in copies:
        copy.wait()


def collect(outputs):
    rows = outputs.shape[1]
    return pl.pallas_call(
        collect_kernel,
        name="collect",
        out_shape=jax.ShapeDtypeStruct((rows, GROUP * WIDE), jnp.bfloat16),
        in_specs=[VMEM],
        out_specs=VMEM,
        scratch_shapes=[
            pltpu.SemaphoreType.DMA,
            pltpu.SemaphoreType.DMA((GROUP,)),
            pltpu.SemaphoreType.DMA((GROUP,)),
        ],
        compiler_params=pltpu.CompilerParams(collective_id=1, has_side_effects=True),
    )(outputs)


def shards(queries, key_row_matrix, values, verticals, slashes, counts):
    assert queries.shape[1] == BLOCK_TOKENS
    groups = lax.axis_size("head") * lax.axis_size("seq") // GROUP
    own, pairs = spread(queries[0], key_row_matrix[0], values[0], groups)
    outputs = attend(verticals, slashes, counts, own, pairs)
    return collect(outputs)[None]


def solution(mesh):
    in_specs = (
        P("seq", "head", None),
        P("seq", "head", None),
        P("seq", "head", None),
        P(),
        P(),
        P(),
    )
    out_specs = P("seq", "head", None)
    return jax.shard_map(shards, mesh=mesh, in_specs=in_specs, out_specs=out_specs, check_vma=False)
```

```python
import functools
import math

import jax
import jax.numpy as jnp
from jax import lax
from jax.experimental import pallas as pl
from jax.experimental.pallas import tpu as pltpu
from jax.sharding import PartitionSpec as P

QUERY_HEADS = 32
KEY_VALUE_HEADS = 8
HEAD_WIDTH = 128
BLOCK_TOKENS = 128
GROUP = KEY_VALUE_HEADS
SHARED = QUERY_HEADS // KEY_VALUE_HEADS
WIDE = SHARED * HEAD_WIDTH
ORDER = (4, 2, 6, 5, 3, 7, 1)
MESH = pl.DeviceIdType.MESH
VMEM = pl.BlockSpec(memory_space=pltpu.VMEM)
SMEM = pl.BlockSpec(memory_space=pltpu.SMEM)


def flipped(member, bits):
    parts = (member % 2, (member // 2) % 2, member // 4)
    return sum(((part + ((bits >> k) & 1)) % 2) * (1 << k) for k, part in enumerate(parts))


def place():
    seqs = lax.axis_size("seq")
    number = lax.axis_index("head") * seqs + lax.axis_index("seq")
    return seqs, number, number // GROUP, number % GROUP


def greet(barrier, seqs, number):
    pl.semaphore_signal(
        barrier, inc=1, device_id=(number // seqs, number % seqs), device_id_type=MESH
    )


def spread_kernel(
    groups, q_in, k_in, v_in, q_out, kv_out, own, kv_send, kv_got, q_send, q_got, z_send, z_got
):
    seqs, me, plane, member = place()
    base = plane * GROUP
    has_above = plane < groups - 1
    has_below = plane > 0
    barrier = pltpu.get_barrier_semaphore()
    for bits in ORDER:
        greet(barrier, seqs, base + flipped(member, bits))

    @pl.when(has_above)
    def _():
        greet(barrier, seqs, me + GROUP)

    @pl.when(has_below)
    def _():
        greet(barrier, seqs, me - GROUP)

    def narrow(ref, to):
        return ref.at[:, pl.ds(pl.multiple_of(to * HEAD_WIDTH, HEAD_WIDTH), HEAD_WIDTH)]

    def wide(ref, to):
        return ref.at[:, pl.ds(pl.multiple_of(to * WIDE, WIDE), WIDE)]

    stay = [
        pltpu.make_async_copy(narrow(k_in, member), kv_out.at[me, 0], own.at[0]),
        pltpu.make_async_copy(narrow(v_in, member), kv_out.at[me, 1], own.at[1]),
        pltpu.make_async_copy(wide(q_in, member), q_out.at[member], own.at[2]),
    ]
    for copy in stay:
        copy.start()
    pl.semaphore_wait(
        barrier, GROUP - 1 + jnp.where(has_above, 1, 0) + jnp.where(has_below, 1, 0)
    )

    def remote(src, dst, send, got, to):
        return pltpu.make_async_remote_copy(
            src_ref=src,
            dst_ref=dst,
            send_sem=send,
            recv_sem=got,
            device_id=(to // seqs, to % seqs),
            device_id_type=MESH,
        )

    kv_copies, q_copies = [], []
    for bits in ORDER:
        to = flipped(member, bits)
        for which, ref in enumerate((k_in, v_in)):
            kv_copies.append(
                remote(
                    narrow(ref, to),
                    kv_out.at[me, which],
                    kv_send.at[which, bits],
                    kv_got.at[which, bits],
                    base + to,
                )
            )
            kv_copies[-1].start()
    def up(block):
        return remote(
            kv_out.at[block], kv_out.at[block], z_send.at[0, block], z_got.at[block], me + GROUP
        )

    def down(block):
        return remote(
            kv_out.at[block], kv_out.at[block], z_send.at[1, block], z_got.at[block], me - GROUP
        )

    def pass_on(block, upward, downward):
        if upward:

            @pl.when(has_above)
            def _():
                up(block).start()

        if downward:

            @pl.when(has_below)
            def _():
                down(block).start()

    stay[0].wait()
    stay[1].wait()
    pass_on(me, True, True)
    for at, bits in enumerate(ORDER):
        kv_copies[2 * at].wait_recv()
        kv_copies[2 * at + 1].wait_recv()
        pass_on(base + flipped(member, bits), True, True)
    for bits in ORDER:
        to = flipped(member, bits)
        q_copies.append(
            remote(wide(q_in, to), q_out.at[member], q_send.at[bits], q_got.at[bits], base + to)
        )
        q_copies[-1].start()

    def far_step(step, carry):
        for bits in (0,) + ORDER:
            other = flipped(member, bits)
            lower = (plane - step) * GROUP + other
            upper = (plane + step) * GROUP + other

            @pl.when(plane - step >= 0)
            def _():
                up(lower).wait_recv()
                pass_on(lower, True, False)

            @pl.when(plane + step < groups)
            def _():
                down(upper).wait_recv()
                pass_on(upper, False, True)

        return carry

    lax.fori_loop(1, groups, far_step, 0)
    stay[2].wait()
    for copy in kv_copies:
        copy.wait_send()
    for copy in q_copies:
        copy.wait()

    def sent_step(step, carry):
        for other in range(GROUP):
            block = step * GROUP + other

            @pl.when(has_above & (step <= plane))
            def _():
                up(block).wait_send()

            @pl.when(has_below & (step >= plane))
            def _():
                down(block).wait_send()

        return carry

    lax.fori_loop(0, groups, sent_step, 0)


def spread(queries, keys, values, groups):
    count = groups * GROUP
    rows = queries.shape[0]
    return pl.pallas_call(
        functools.partial(spread_kernel, groups),
        name="spread",
        out_shape=(
            jax.ShapeDtypeStruct((GROUP, rows, WIDE), jnp.bfloat16),
            jax.ShapeDtypeStruct((count, 2, rows, HEAD_WIDTH), jnp.bfloat16),
        ),
        in_specs=[VMEM] * 3,
        out_specs=(VMEM, VMEM),
        scratch_shapes=[
            pltpu.SemaphoreType.DMA((3,)),
            pltpu.SemaphoreType.DMA((2, GROUP)),
            pltpu.SemaphoreType.DMA((2, GROUP)),
            pltpu.SemaphoreType.DMA((GROUP,)),
            pltpu.SemaphoreType.DMA((GROUP,)),
            pltpu.SemaphoreType.DMA((2, count)),
            pltpu.SemaphoreType.DMA((count,)),
        ],
        compiler_params=pltpu.CompilerParams(collective_id=0, has_side_effects=True),
    )(queries, keys, values)


def attend_kernel(verticals, slashes, counts, q, kv, out, scores, top, total, mixed):
    heads = lax.axis_size("head")
    seqs, me, plane, member = place()
    base = plane * GROUP
    slash_slots = slashes.shape[0]
    factor = math.log2(math.e) / math.sqrt(HEAD_WIDTH)
    rows = lax.broadcasted_iota(jnp.int32, (BLOCK_TOKENS, BLOCK_TOKENS), 0)
    cols = lax.broadcasted_iota(jnp.int32, (BLOCK_TOKENS, BLOCK_TOKENS), 1)
    causal = rows >= cols
    block_ids = [
        ((base + t) % seqs) * heads + (base + t) // seqs for t in range(GROUP)
    ]

    def holder(block):
        return (block % heads) * seqs + block // heads

    def product(left, right, dims):
        return lax.dot_general(left, right, (dims, ((), ())), preferred_element_type=jnp.float32)

    def one_head(j, carry):
        head = member * SHARED + j
        columns = pl.ds(pl.multiple_of(j * HEAD_WIDTH, HEAD_WIDTH), HEAD_WIDTH)
        n_slash = counts[1, head]
        n_column = counts[0, head]

        def keep(slot, t, key, active):
            found = product(q[t, :, columns], key, ((1,), (1,)))
            found = jnp.where(active, found, -jnp.inf)
            scores[slot, t] = found
            top[t] = jnp.maximum(top[t], found)

        for t in range(GROUP):
            found = product(q[t, :, columns], kv[base + t, 0], ((1,), (1,)))
            found = jnp.where(causal, found, -jnp.inf)
            scores[0, t] = found
            top[t] = found

        def slash_scores(slot, carry):
            offset = slashes[slot, head]
            for t in range(GROUP):
                block = block_ids[t] - offset
                keep(1 + slot, t, kv[holder(jnp.maximum(block, 0)), 0], block >= 0)
            return carry

        def column_scores(slot, carry):
            column = verticals[slot, head]
            key = kv[holder(column), 0]
            for t in range(GROUP):
                active = column < block_ids[t]
                for s in range(slash_slots):
                    repeated = (block_ids[t] - column == slashes[s, head]) & (s < n_slash)
                    active = active & jnp.logical_not(repeated)
                keep(1 + n_slash + slot, t, key, active)
            return carry

        lax.fori_loop(0, n_slash, slash_scores, 0)
        lax.fori_loop(0, n_column, column_scores, 0)

        def weigh(slot, t, first, value):
            weights = jnp.exp2((scores[slot, t] - top[t]) * factor)
            part = product(weights.astype(jnp.bfloat16), value, ((1,), (0,)))
            if first:
                total[t] = weights
                mixed[t] = part
            else:
                total[t] = total[t] + weights
                mixed[t] = mixed[t] + part

        for t in range(GROUP):
            top[t] = jnp.broadcast_to(jnp.max(top[t], axis=1, keepdims=True), top.shape[1:])
        for t in range(GROUP):
            weigh(0, t, True, kv[base + t, 1])

        def slash_mix(slot, carry):
            offset = slashes[slot, head]
            for t in range(GROUP):
                block = jnp.maximum(block_ids[t] - offset, 0)
                weigh(1 + slot, t, False, kv[holder(block), 1])
            return carry

        def column_mix(slot, carry):
            value = kv[holder(verticals[slot, head]), 1]
            for t in range(GROUP):
                weigh(1 + n_slash + slot, t, False, value)
            return carry

        lax.fori_loop(0, n_slash, slash_mix, 0)
        lax.fori_loop(0, n_column, column_mix, 0)
        for t in range(GROUP):
            sums = jnp.sum(total[t], axis=1, keepdims=True)
            out[t, :, columns] = (mixed[t] / sums).astype(out.dtype)
        return carry

    lax.fori_loop(0, SHARED, one_head, 0)


def attend(verticals, slashes, counts, queries, pairs):
    slots = 1 + verticals.shape[0] + slashes.shape[0]
    tile = (BLOCK_TOKENS, BLOCK_TOKENS)
    return pl.pallas_call(
        attend_kernel,
        name="attend",
        out_shape=jax.ShapeDtypeStruct(queries.shape, jnp.bfloat16),
        in_specs=[SMEM] * 3 + [VMEM] * 2,
        out_specs=VMEM,
        scratch_shapes=[
            pltpu.VMEM((slots, GROUP) + tile, jnp.float32),
            pltpu.VMEM((GROUP,) + tile, jnp.float32),
            pltpu.VMEM((GROUP,) + tile, jnp.float32),
            pltpu.VMEM((GROUP,) + tile, jnp.float32),
        ],
    )(verticals, slashes, counts, queries, pairs)


def collect_kernel(o_in, out, own, send, got):
    seqs, me, plane, member = place()
    base = plane * GROUP
    barrier = pltpu.get_barrier_semaphore()
    for bits in ORDER:
        greet(barrier, seqs, base + flipped(member, bits))
    mine = out.at[:, pl.ds(pl.multiple_of(member * WIDE, WIDE), WIDE)]
    stay = pltpu.make_async_copy(o_in.at[member], mine, own)
    stay.start()
    pl.semaphore_wait(barrier, GROUP - 1)
    copies = []
    for bits in ORDER:
        to = flipped(member, bits)
        copies.append(
            pltpu.make_async_remote_copy(
                src_ref=o_in.at[to],
                dst_ref=mine,
                send_sem=send.at[bits],
                recv_sem=got.at[bits],
                device_id=((base + to) // seqs, (base + to) % seqs),
                device_id_type=MESH,
            )
        )
        copies[-1].start()
    stay.wait()
    for copy in copies:
        copy.wait()


def collect(outputs):
    rows = outputs.shape[1]
    return pl.pallas_call(
        collect_kernel,
        name="collect",
        out_shape=jax.ShapeDtypeStruct((rows, GROUP * WIDE), jnp.bfloat16),
        in_specs=[VMEM],
        out_specs=VMEM,
        scratch_shapes=[
            pltpu.SemaphoreType.DMA,
            pltpu.SemaphoreType.DMA((GROUP,)),
            pltpu.SemaphoreType.DMA((GROUP,)),
        ],
        compiler_params=pltpu.CompilerParams(collective_id=1, has_side_effects=True),
    )(outputs)


def shards(queries, key_row_matrix, values, verticals, slashes, counts):
    assert queries.shape[1] == BLOCK_TOKENS
    groups = lax.axis_size("head") * lax.axis_size("seq") // GROUP
    own, pairs = spread(queries[0], key_row_matrix[0], values[0], groups)
    outputs = attend(verticals.T, slashes.T, counts.T, own, pairs)
    return collect(outputs)[None]


def solution(mesh):
    in_specs = (
        P("seq", "head", None),
        P("seq", "head", None),
        P("seq", "head", None),
        P(),
        P(),
        P(),
    )
    out_specs = P("seq", "head", None)
    return jax.shard_map(shards, mesh=mesh, in_specs=in_specs, out_specs=out_specs, check_vma=False)
```

```python
import functools
import math

import jax
import jax.numpy as jnp
from jax import lax
from jax.experimental import pallas as pl
from jax.experimental.pallas import tpu as pltpu
from jax.sharding import PartitionSpec as P

QUERY_HEADS = 32
KEY_VALUE_HEADS = 8
HEAD_WIDTH = 128
BLOCK_TOKENS = 128
GROUP = KEY_VALUE_HEADS
SHARED = QUERY_HEADS // KEY_VALUE_HEADS
WIDE = SHARED * HEAD_WIDTH
ORDER = (4, 2, 6, 5, 3, 7, 1)
MESH = pl.DeviceIdType.MESH
ANY = pl.BlockSpec(memory_space=pl.ANY)
VMEM_BYTES = 62 * 1024 * 1024
SMEM = pl.BlockSpec(memory_space=pltpu.SMEM)


def flipped(member, bits):
    parts = (member % 2, (member // 2) % 2, member // 4)
    return sum(((part + ((bits >> k) & 1)) % 2) * (1 << k) for k, part in enumerate(parts))


def flipped_by(member, bits):
    total = 0
    for size in (1, 2, 4):
        total += lax.rem(lax.div(member, size) + lax.div(bits, size), 2) * size
    return total


def place():
    seqs = lax.axis_size("seq")
    number = lax.axis_index("head") * seqs + lax.axis_index("seq")
    return seqs, number, number // GROUP, number % GROUP


def greet(barrier, seqs, number):
    pl.semaphore_signal(
        barrier, inc=1, device_id=(number // seqs, number % seqs), device_id_type=MESH
    )


def kernel(
    groups, verticals, slashes, counts, q_in, k_in, v_in, out, queries, keys, values, scores, top,
    results, own, kv_send, kv_got, q_send, q_got, k_pass, k_got, v_pass, v_got, o_send, o_got
):
    heads = lax.axis_size("head")
    seqs, me, plane, member = place()
    base = plane * GROUP
    has_above = plane < groups - 1
    has_below = plane > 0
    barrier = pltpu.get_barrier_semaphore()
    for bits in ORDER:
        greet(barrier, seqs, base + flipped(member, bits))

    @pl.when(has_above)
    def _():
        greet(barrier, seqs, me + GROUP)

    @pl.when(has_below)
    def _():
        greet(barrier, seqs, me - GROUP)

    def narrow(ref, to):
        return ref.at[:, pl.ds(pl.multiple_of(to * HEAD_WIDTH, HEAD_WIDTH), HEAD_WIDTH)]

    def wide(ref, to):
        return ref.at[:, pl.ds(pl.multiple_of(to * WIDE, WIDE), WIDE)]

    def remote(src, dst, send, got, to):
        return pltpu.make_async_remote_copy(
            src_ref=src,
            dst_ref=dst,
            send_sem=send,
            recv_sem=got,
            device_id=(to // seqs, to % seqs),
            device_id_type=MESH,
        )

    stay = [
        pltpu.make_async_copy(narrow(k_in, member), keys.at[me], own.at[0]),
        pltpu.make_async_copy(narrow(v_in, member), values.at[me], own.at[1]),
        pltpu.make_async_copy(wide(q_in, member), queries.at[member], own.at[2]),
    ]
    for copy in stay:
        copy.start()
    pl.semaphore_wait(
        barrier, GROUP - 1 + jnp.where(has_above, 1, 0) + jnp.where(has_below, 1, 0)
    )
    near = ([], [], [])
    for which, (ref, kept) in enumerate(((k_in, keys), (v_in, values))):
        for bits in ORDER:
            to = flipped(member, bits)
            near[which].append(
                remote(
                    narrow(ref, to),
                    kept.at[me],
                    kv_send.at[which, bits],
                    kv_got.at[which, bits],
                    base + to,
                )
            )
            near[which][-1].start()
    for bits in ORDER:
        to = flipped(member, bits)
        near[2].append(
            remote(wide(q_in, to), queries.at[member], q_send.at[bits], q_got.at[bits], base + to)
        )
        near[2][-1].start()

    def relay(ref, send, got):
        def up(block):
            return remote(ref.at[block], ref.at[block], send.at[0, block], got.at[block], me + GROUP)

        def down(block):
            return remote(ref.at[block], ref.at[block], send.at[1, block], got.at[block], me - GROUP)

        def pass_on(block, upward, downward):
            if upward:

                @pl.when(has_above)
                def _():
                    up(block).start()

            if downward:

                @pl.when(has_below)
                def _():
                    down(block).start()

        def far(step, bits):
            other = flipped_by(member, bits)
            lower = (plane - step) * GROUP + other
            upper = (plane + step) * GROUP + other

            @pl.when(plane - step >= 0)
            def _():
                up(lower).wait_recv()
                pass_on(lower, True, False)

            @pl.when(plane + step < groups)
            def _():
                down(upper).wait_recv()
                pass_on(upper, False, True)

        def sent(step, carry):
            for other in range(GROUP):
                block = step * GROUP + other

                @pl.when(has_above & (step <= plane))
                def _():
                    up(block).wait_send()

                @pl.when(has_below & (step >= plane))
                def _():
                    down(block).wait_send()

            return carry

        return pass_on, far, sent

    def start_relay(which, pass_on):
        stay[which].wait()
        pass_on(me, True, True)
        for at, bits in enumerate(ORDER):
            near[which][at].wait_recv()
            pass_on(base + flipped(member, bits), True, True)

    k_on, k_far, k_sent = relay(keys, k_pass, k_got)
    v_on, v_far, v_sent = relay(values, v_pass, v_got)

    slash_slots = slashes.shape[0]
    column_slots = verticals.shape[0]
    factor = math.log2(math.e) / math.sqrt(HEAD_WIDTH)
    units = SHARED * GROUP
    steps = (groups - 1) * GROUP

    def holder(block):
        return lax.rem(block, heads) * seqs + lax.div(block, heads)

    def product(left, right, dims):
        return lax.dot_general(left, right, (dims, ((), ())), preferred_element_type=jnp.float32)

    def unit_facts(unit):
        head = member * SHARED + unit // GROUP
        number = base + unit % GROUP
        return head, number, lax.rem(number, seqs) * heads + lax.div(number, seqs)

    def score_unit(unit):
        head, number, block = unit_facts(unit)
        at = pl.multiple_of(unit // GROUP * HEAD_WIDTH, HEAD_WIDTH)
        query = queries[unit % GROUP, :, pl.ds(at, HEAD_WIDTH)]
        rows = lax.broadcasted_iota(jnp.int32, (BLOCK_TOKENS, BLOCK_TOKENS), 0)
        cols = lax.broadcasted_iota(jnp.int32, (BLOCK_TOKENS, BLOCK_TOKENS), 1)
        best = product(query, keys[number], ((1,), (1,)))
        best = jnp.where(rows >= cols, best, -jnp.inf)
        scores[unit, 0] = best
        for slot in range(slash_slots):
            other = block - slashes[slot, head]
            active = (other >= 0) & (slot < counts[1, head])
            found = product(query, keys[holder(jnp.maximum(other, 0))], ((1,), (1,)))
            found = jnp.where(active, found, -jnp.inf)
            scores[unit, 1 + slot] = found
            best = jnp.maximum(best, found)
        for slot in range(column_slots):
            column = verticals[slot, head]
            active = (column < block) & (slot < counts[0, head])
            for s in range(slash_slots):
                repeated = (block - column == slashes[s, head]) & (s < counts[1, head])
                active = active & jnp.logical_not(repeated)
            found = product(query, keys[holder(column)], ((1,), (1,)))
            found = jnp.where(active, found, -jnp.inf)
            scores[unit, 1 + slash_slots + slot] = found
            best = jnp.maximum(best, found)
        top[unit] = jnp.broadcast_to(jnp.max(best, axis=1, keepdims=True), top.shape[1:])

    def mix_unit(unit):
        head, number, block = unit_facts(unit)
        places = [number]
        for slot in range(slash_slots):
            places.append(holder(jnp.maximum(block - slashes[slot, head], 0)))
        for slot in range(column_slots):
            places.append(holder(verticals[slot, head]))
        total = mixed = None
        for slot, at in enumerate(places):
            weights = jnp.exp2((scores[unit, slot] - top[unit]) * factor)
            part = product(weights.astype(jnp.bfloat16), values[at], ((1,), (0,)))
            total = weights if total is None else total + weights
            mixed = part if mixed is None else mixed + part
        mixed = mixed / jnp.sum(total, axis=1, keepdims=True)
        results[unit] = mixed.astype(jnp.bfloat16)

    start_relay(0, k_on)

    def k_step(n, carry):
        k_far(n // GROUP + 1, n % GROUP)
        return carry

    lax.fori_loop(0, steps, k_step, 0)
    start_relay(1, v_on)
    stay[2].wait()
    for copy in near[2]:
        copy.wait_recv()
    lead = max(units - steps, 0)

    def lead_step(n, carry):
        score_unit(n)
        return carry

    def v_step(n, carry):
        if lead + steps == units:
            score_unit(lead + n)
        else:

            @pl.when(n < units)
            def _():
                score_unit(n)

        v_far(n // GROUP + 1, n % GROUP)
        return carry

    lax.fori_loop(0, lead, lead_step, 0)
    lax.fori_loop(0, steps, v_step, 0)

    def unit_of(n):
        return (n // GROUP) * GROUP + flipped_by(member, n % GROUP)

    def column_of(ref, j):
        at = pl.multiple_of((member * SHARED + j) * HEAD_WIDTH, HEAD_WIDTH)
        return ref.at[:, pl.ds(at, HEAD_WIDTH)]

    def give(n):
        j, bits = n // GROUP, n % GROUP
        unit = unit_of(n)
        return remote(
            results.at[unit],
            column_of(out, j),
            o_send.at[j, bits],
            o_got.at[j, bits],
            base + flipped_by(member, bits),
        )

    def take(j, bits):
        owner = flipped_by(member, bits)
        at = pl.multiple_of((owner * SHARED + j) * HEAD_WIDTH, HEAD_WIDTH)
        return remote(
            results.at[j * GROUP],
            out.at[:, pl.ds(at, HEAD_WIDTH)],
            o_send.at[j, bits],
            o_got.at[j, bits],
            base + owner,
        )

    def hold(j):
        return pltpu.make_async_copy(
            results.at[j * GROUP + member], column_of(out, j), own.at[3 + j]
        )

    def hand_out(n):
        @pl.when(n % GROUP > 0)
        def _():
            give(n).start()

        @pl.when(n % GROUP == 0)
        def _():
            hold(n // GROUP).start()

    def mix_step(n, carry):
        mix_unit(unit_of(2 * n))
        mix_unit(unit_of(2 * n + 1))

        @pl.when(n > 0)
        def _():
            hand_out(2 * n - 2)
            hand_out(2 * n - 1)

        return carry

    lax.fori_loop(0, units // 2, mix_step, 0)
    hand_out(units - 2)
    hand_out(units - 1)
    for which in range(3):
        for copy in near[which]:
            copy.wait_send()
    lax.fori_loop(0, groups, k_sent, 0)
    lax.fori_loop(0, groups, v_sent, 0)
    for j in range(SHARED):
        hold(j).wait()
        for bits in ORDER:
            give(j * GROUP + bits).wait_send()
            take(j, bits).wait_recv()


def shards(queries, key_row_matrix, values, verticals, slashes, counts):
    rows, width = queries.shape[1:]
    assert rows == BLOCK_TOKENS
    groups = lax.axis_size("head") * lax.axis_size("seq") // GROUP
    count = groups * GROUP
    units = SHARED * GROUP
    slots = 1 + verticals.shape[1] + slashes.shape[1]
    block = (BLOCK_TOKENS, HEAD_WIDTH)
    out = pl.pallas_call(
        functools.partial(kernel, groups),
        name="block_sparse_attention",
        out_shape=jax.ShapeDtypeStruct((rows, width), jnp.bfloat16),
        in_specs=[SMEM] * 3 + [ANY] * 3,
        out_specs=ANY,
        scratch_shapes=[
            pltpu.VMEM((GROUP, rows, WIDE), jnp.bfloat16),
            pltpu.VMEM((count,) + block, jnp.bfloat16),
            pltpu.VMEM((count,) + block, jnp.bfloat16),
            pltpu.VMEM((units, slots, BLOCK_TOKENS, BLOCK_TOKENS), jnp.float32),
            pltpu.VMEM((units, BLOCK_TOKENS, BLOCK_TOKENS), jnp.float32),
            pltpu.VMEM((units,) + block, jnp.bfloat16),
            pltpu.SemaphoreType.DMA((3 + SHARED,)),
            pltpu.SemaphoreType.DMA((2, GROUP)),
            pltpu.SemaphoreType.DMA((2, GROUP)),
            pltpu.SemaphoreType.DMA((GROUP,)),
            pltpu.SemaphoreType.DMA((GROUP,)),
            pltpu.SemaphoreType.DMA((2, count)),
            pltpu.SemaphoreType.DMA((count,)),
            pltpu.SemaphoreType.DMA((2, count)),
            pltpu.SemaphoreType.DMA((count,)),
            pltpu.SemaphoreType.DMA((SHARED, GROUP)),
            pltpu.SemaphoreType.DMA((SHARED, GROUP)),
        ],
        compiler_params=pltpu.CompilerParams(
            collective_id=0, has_side_effects=True, vmem_limit_bytes=VMEM_BYTES
        ),
    )(verticals.T, slashes.T, counts.T, queries[0], key_row_matrix[0], values[0])
    return out[None]


def solution(mesh):
    in_specs = (
        P("seq", "head", None),
        P("seq", "head", None),
        P("seq", "head", None),
        P(),
        P(),
        P(),
    )
    out_specs = P("seq", "head", None)
    return jax.shard_map(shards, mesh=mesh, in_specs=in_specs, out_specs=out_specs, check_vma=False)
```

```python
import functools
import math

import jax
import jax.numpy as jnp
from jax import lax
from jax.experimental import pallas as pl
from jax.experimental.pallas import tpu as pltpu
from jax.sharding import PartitionSpec as P

QUERY_HEADS = 32
KEY_VALUE_HEADS = 8
HEAD_WIDTH = 128
BLOCK_TOKENS = 128
GROUP = KEY_VALUE_HEADS
SHARED = QUERY_HEADS // KEY_VALUE_HEADS
WIDE = SHARED * HEAD_WIDTH
ORDER = (4, 2, 6, 5, 3, 7, 1)
MESH = pl.DeviceIdType.MESH
ANY = pl.BlockSpec(memory_space=pl.ANY)
VMEM_BYTES = 62 * 1024 * 1024
SMEM = pl.BlockSpec(memory_space=pltpu.SMEM)


def flipped(member, bits):
    parts = (member % 2, (member // 2) % 2, member // 4)
    return sum(((part + ((bits >> k) & 1)) % 2) * (1 << k) for k, part in enumerate(parts))


def stages_for(seqs):
    return seqs if GROUP % seqs == 0 else 1


def place():
    seqs = lax.axis_size("seq")
    number = lax.axis_index("head") * seqs + lax.axis_index("seq")
    return seqs, number, number // GROUP, number % GROUP


def greet(barrier, seqs, number):
    pl.semaphore_signal(
        barrier, inc=1, device_id=(number // seqs, number % seqs), device_id_type=MESH
    )


def kernel(
    groups, verticals, slashes, counts, q_in, k_in, v_in, out, queries, keys, values, scores, top,
    results, seen_keys, seen_values, own, kv_send, kv_got, q_send, q_got, k_pass, k_got, v_pass, v_got, o_send, o_got
):
    heads = lax.axis_size("head")
    seqs, me, plane, member = place()
    base = plane * GROUP
    has_above = plane < groups - 1
    has_below = plane > 0
    barrier = pltpu.get_barrier_semaphore()
    for bits in ORDER:
        greet(barrier, seqs, base + flipped(member, bits))

    @pl.when(has_above)
    def _():
        greet(barrier, seqs, me + GROUP)

    @pl.when(has_below)
    def _():
        greet(barrier, seqs, me - GROUP)

    def narrow(ref, to):
        return ref.at[:, pl.ds(pl.multiple_of(to * HEAD_WIDTH, HEAD_WIDTH), HEAD_WIDTH)]

    def wide(ref, to):
        return ref.at[:, pl.ds(pl.multiple_of(to * WIDE, WIDE), WIDE)]

    def remote(src, dst, send, got, to):
        return pltpu.make_async_remote_copy(
            src_ref=src,
            dst_ref=dst,
            send_sem=send,
            recv_sem=got,
            device_id=(to // seqs, to % seqs),
            device_id_type=MESH,
        )

    stay = [
        pltpu.make_async_copy(narrow(k_in, member), keys.at[me], own.at[0]),
        pltpu.make_async_copy(narrow(v_in, member), values.at[me], own.at[1]),
        pltpu.make_async_copy(wide(q_in, member), queries.at[member], own.at[2]),
    ]
    for copy in stay:
        copy.start()
    pl.semaphore_wait(
        barrier, GROUP - 1 + jnp.where(has_above, 1, 0) + jnp.where(has_below, 1, 0)
    )
    stages = stages_for(seqs)
    each = GROUP // stages

    def near_kv(which, owner, to):
        ref, kept = ((k_in, keys), (v_in, values))[which]
        return remote(
            narrow(ref, to),
            kept.at[base + owner],
            kv_send.at[which, to],
            kv_got.at[which, owner],
            base + to,
        )

    def near_q(owner, to):
        return remote(
            wide(q_in, to), queries.at[owner], q_send.at[to], q_got.at[owner], base + to
        )

    for which in range(2):
        for bits in ORDER:
            near_kv(which, member, flipped(member, bits)).start()
    for bits in ORDER:
        near_q(member, flipped(member, bits)).start()

    def relay(ref, send, got):
        def up(block):
            return remote(ref.at[block], ref.at[block], send.at[0, block], got.at[block], me + GROUP)

        def down(block):
            return remote(ref.at[block], ref.at[block], send.at[1, block], got.at[block], me - GROUP)

        def pass_on(block, upward, downward):
            if upward:

                @pl.when(has_above)
                def _():
                    up(block).start()

            if downward:

                @pl.when(has_below)
                def _():
                    down(block).start()

        def far(step, other):
            lower = (plane - step) * GROUP + other
            upper = (plane + step) * GROUP + other

            @pl.when(plane - step >= 0)
            def _():
                up(lower).wait_recv()
                pass_on(lower, True, False)

            @pl.when(plane + step < groups)
            def _():
                down(upper).wait_recv()
                pass_on(upper, False, True)

        def sent(step, carry):
            for other in range(GROUP):
                block = step * GROUP + other

                @pl.when(has_above & (step <= plane))
                def _():
                    up(block).wait_send()

                @pl.when(has_below & (step >= plane))
                def _():
                    down(block).wait_send()

            return carry

        return pass_on, far, sent

    k_relay = relay(keys, k_pass, k_got)
    v_relay = relay(values, v_pass, v_got)

    def set_off(phase):
        stage, which = phase // 2, phase % 2
        for i in range(each):
            t = stage + stages * i

            @pl.when(member == t)
            def _():
                stay[which].wait()

            @pl.when(member != t)
            def _():
                near_kv(which, t, t).wait_recv()

            (k_relay, v_relay)[which][0](base + t, True, True)

    def note(phase):
        if stages == 1:
            return
        stage, which = phase // 2, phase % 2
        kept, seen = ((keys, seen_keys), (values, seen_values))[which]

        def note_step(n, carry):
            at = (n // each) * GROUP + stage + stages * (n % each)
            seen[at] = kept[at]
            return carry

        lax.fori_loop(0, groups * each, note_step, 0)

    slash_slots = slashes.shape[0]
    column_slots = verticals.shape[0]
    factor = math.log2(math.e) / math.sqrt(HEAD_WIDTH)
    key_blocks, value_blocks = (keys, values) if stages == 1 else (seen_keys, seen_values)
    in_stage = SHARED * each
    steps = (groups - 1) * each

    def holder(block):
        return lax.rem(block, heads) * seqs + lax.div(block, heads)

    def product(left, right, dims):
        return lax.dot_general(left, right, (dims, ((), ())), preferred_element_type=jnp.float32)

    def unit_facts(unit):
        head = member * SHARED + unit // GROUP
        number = base + unit % GROUP
        return head, number, lax.rem(number, seqs) * heads + lax.div(number, seqs)

    def score_unit(unit):
        head, number, block = unit_facts(unit)
        at = pl.multiple_of(unit // GROUP * HEAD_WIDTH, HEAD_WIDTH)
        query = queries[unit % GROUP, :, pl.ds(at, HEAD_WIDTH)]
        rows = lax.broadcasted_iota(jnp.int32, (BLOCK_TOKENS, BLOCK_TOKENS), 0)
        cols = lax.broadcasted_iota(jnp.int32, (BLOCK_TOKENS, BLOCK_TOKENS), 1)
        best = product(query, key_blocks[number], ((1,), (1,)))
        best = jnp.where(rows >= cols, best, -jnp.inf)
        scores[unit, 0] = best
        for slot in range(slash_slots):
            other = block - slashes[slot, head]
            active = (other >= 0) & (slot < counts[1, head])
            found = product(query, key_blocks[holder(jnp.maximum(other, 0))], ((1,), (1,)))
            found = jnp.where(active, found, -jnp.inf)
            scores[unit, 1 + slot] = found
            best = jnp.maximum(best, found)
        for slot in range(column_slots):
            column = verticals[slot, head]
            active = (column < block) & (slot < counts[0, head])
            for s in range(slash_slots):
                repeated = (block - column == slashes[s, head]) & (s < counts[1, head])
                active = active & jnp.logical_not(repeated)
            found = product(query, key_blocks[holder(jnp.minimum(column, block))], ((1,), (1,)))
            found = jnp.where(active, found, -jnp.inf)
            scores[unit, 1 + slash_slots + slot] = found
            best = jnp.maximum(best, found)
        top[unit] = jnp.broadcast_to(jnp.max(best, axis=1, keepdims=True), top.shape[1:])

    def mix_unit(unit):
        head, number, block = unit_facts(unit)
        places = [number]
        for slot in range(slash_slots):
            places.append(holder(jnp.maximum(block - slashes[slot, head], 0)))
        for slot in range(column_slots):
            places.append(holder(jnp.minimum(verticals[slot, head], block)))
        total = mixed = None
        for slot, at in enumerate(places):
            weights = jnp.exp2((scores[unit, slot] - top[unit]) * factor)
            part = product(weights.astype(jnp.bfloat16), value_blocks[at], ((1,), (0,)))
            total = weights if total is None else total + weights
            mixed = part if mixed is None else mixed + part
        mixed = mixed / jnp.sum(total, axis=1, keepdims=True)
        results[unit] = mixed.astype(jnp.bfloat16)

    def unit_in(stage, n):
        return n // each * GROUP + stage + stages * (n % each)

    def column_of(ref, owner, j):
        at = pl.multiple_of((owner * SHARED + j) * HEAD_WIDTH, HEAD_WIDTH)
        return ref.at[:, pl.ds(at, HEAD_WIDTH)]

    def give(j, owner, t):
        return remote(
            results.at[j * GROUP + t],
            column_of(out, owner, j),
            o_send.at[j, t],
            o_got.at[j, owner],
            base + t,
        )

    def hold(j):
        return pltpu.make_async_copy(
            results.at[j * GROUP + member], column_of(out, member, j), own.at[3 + j]
        )

    def hand_out(unit):
        j, t = unit // GROUP, unit % GROUP

        @pl.when(t != member)
        def _():
            give(j, member, t).start()

        @pl.when(t == member)
        def _():
            hold(j).start()

    def q_ready(stage):
        for i in range(each):
            t = stage + stages * i

            @pl.when(member == t)
            def _():
                stay[2].wait()

            @pl.when(member != t)
            def _():
                near_q(t, t).wait_recv()

    def between(far, first, count, total, work, after):
        def piece(n, carry):
            start, stop = n * total // count, (n + 1) * total // count

            def inner(u, carry):
                work(u)
                return carry

            lax.fori_loop(start, stop, inner, 0)
            far(first + n)
            if after is not None:

                def later(u, carry):
                    after(u)
                    return carry

                lax.fori_loop(start, stop, later, 0)
            return carry

        lax.fori_loop(0, count, piece, 0)

    def job_of(kind, stage):
        if kind == 0:
            return in_stage, (lambda u: score_unit(unit_in(stage, u))), None

        def mix(u):
            mix_unit(unit_in(stage, 2 * u))
            mix_unit(unit_in(stage, 2 * u + 1))

        def send(u):
            hand_out(unit_in(stage, 2 * u))
            hand_out(unit_in(stage, 2 * u + 1))

        return in_stage // 2, mix, send

    phases = 2 * stages
    jobs = [(kind, stage) for stage in range(stages) for kind in range(2)]
    opening = min(3, phases - 1)
    set_off(0)
    for phase in range(phases):
        stage, which = phase // 2, phase % 2
        if phase + 1 < phases:
            set_off(phase + 1)
        far_step = (k_relay, v_relay)[which][1]

        def far(n, far_step=far_step, stage=stage):
            far_step(n // each + 1, stage + stages * (n % each))

        now = []
        while phase >= opening and len(now) < 2 and jobs and 2 * jobs[0][1] + jobs[0][0] < phase:
            now.append(jobs.pop(0))
        done = 0
        for at, (kind, work_stage) in enumerate(now):
            if kind == 0:
                q_ready(work_stage)
            share = steps * (at + 1) // len(now) - done
            between(far, done, share, *job_of(kind, work_stage))
            done += share
        if not now:
            between(far, 0, steps, 0, lambda u: None, None)
        note(phase)
    for kind, stage in jobs:
        total, work, after = job_of(kind, stage)
        if kind == 0:
            q_ready(stage)

        def last(n, carry, work=work, after=after):
            work(n)
            if after is not None:

                @pl.when(n > 0)
                def _():
                    after(n - 1)

            return carry

        lax.fori_loop(0, total, last, 0)
        if after is not None:
            after(total - 1)
    for bits in ORDER:
        to = flipped(member, bits)
        near_kv(0, member, to).wait_send()
        near_kv(1, member, to).wait_send()
        near_q(member, to).wait_send()
    lax.fori_loop(0, groups, k_relay[2], 0)
    lax.fori_loop(0, groups, v_relay[2], 0)
    for j in range(SHARED):
        hold(j).wait()
        for bits in ORDER:
            other = flipped(member, bits)
            give(j, member, other).wait_send()
            give(j, other, other).wait_recv()


def shards(queries, key_row_matrix, values, verticals, slashes, counts):
    rows, width = queries.shape[1:]
    assert rows == BLOCK_TOKENS
    groups = lax.axis_size("head") * lax.axis_size("seq") // GROUP
    count = groups * GROUP
    units = SHARED * GROUP
    slots = 1 + verticals.shape[1] + slashes.shape[1]
    block = (BLOCK_TOKENS, HEAD_WIDTH)
    seen = count if stages_for(lax.axis_size("seq")) > 1 else 1
    out = pl.pallas_call(
        functools.partial(kernel, groups),
        name="block_sparse_attention",
        out_shape=jax.ShapeDtypeStruct((rows, width), jnp.bfloat16),
        in_specs=[SMEM] * 3 + [ANY] * 3,
        out_specs=ANY,
        scratch_shapes=[
            pltpu.VMEM((GROUP, rows, WIDE), jnp.bfloat16),
            pltpu.VMEM((count,) + block, jnp.bfloat16),
            pltpu.VMEM((count,) + block, jnp.bfloat16),
            pltpu.VMEM((units, slots, BLOCK_TOKENS, BLOCK_TOKENS), jnp.float32),
            pltpu.VMEM((units, BLOCK_TOKENS, BLOCK_TOKENS), jnp.float32),
            pltpu.VMEM((units,) + block, jnp.bfloat16),
            pltpu.VMEM((seen,) + block, jnp.bfloat16),
            pltpu.VMEM((seen,) + block, jnp.bfloat16),
            pltpu.SemaphoreType.DMA((3 + SHARED,)),
            pltpu.SemaphoreType.DMA((2, GROUP)),
            pltpu.SemaphoreType.DMA((2, GROUP)),
            pltpu.SemaphoreType.DMA((GROUP,)),
            pltpu.SemaphoreType.DMA((GROUP,)),
            pltpu.SemaphoreType.DMA((2, count)),
            pltpu.SemaphoreType.DMA((count,)),
            pltpu.SemaphoreType.DMA((2, count)),
            pltpu.SemaphoreType.DMA((count,)),
            pltpu.SemaphoreType.DMA((SHARED, GROUP)),
            pltpu.SemaphoreType.DMA((SHARED, GROUP)),
        ],
        compiler_params=pltpu.CompilerParams(
            collective_id=0, has_side_effects=True, vmem_limit_bytes=VMEM_BYTES
        ),
    )(verticals.T, slashes.T, counts.T, queries[0], key_row_matrix[0], values[0])
    return out[None]


def solution(mesh):
    in_specs = (
        P("seq", "head", None),
        P("seq", "head", None),
        P("seq", "head", None),
        P(),
        P(),
        P(),
    )
    out_specs = P("seq", "head", None)
    return jax.shard_map(shards, mesh=mesh, in_specs=in_specs, out_specs=out_specs, check_vma=False)
```

```python
import functools
import math

import jax
import jax.numpy as jnp
from jax import lax
from jax.experimental import pallas as pl
from jax.experimental.pallas import tpu as pltpu
from jax.sharding import PartitionSpec as P

QUERY_HEADS = 32
KEY_VALUE_HEADS = 8
HEAD_WIDTH = 128
BLOCK_TOKENS = 128
GROUP = KEY_VALUE_HEADS
SHARED = QUERY_HEADS // KEY_VALUE_HEADS
WIDE = SHARED * HEAD_WIDTH
ORDER = (4, 2, 6, 5, 3, 7, 1)
MESH = pl.DeviceIdType.MESH
ANY = pl.BlockSpec(memory_space=pl.ANY)
VMEM_BYTES = 62 * 1024 * 1024
SMEM = pl.BlockSpec(memory_space=pltpu.SMEM)


def flipped(member, bits):
    parts = (member % 2, (member // 2) % 2, member // 4)
    return sum(((part + ((bits >> k) & 1)) % 2) * (1 << k) for k, part in enumerate(parts))


def stages_for(seqs):
    return seqs if GROUP % seqs == 0 else 1


def place():
    seqs = lax.axis_size("seq")
    number = lax.axis_index("head") * seqs + lax.axis_index("seq")
    return seqs, number, number // GROUP, number % GROUP


def greet(barrier, seqs, number):
    pl.semaphore_signal(
        barrier, inc=1, device_id=(number // seqs, number % seqs), device_id_type=MESH
    )


def kernel(
    groups, verticals, slashes, counts, q_in, k_in, v_in, out, queries, keys, values, scores, top,
    results, seen_keys, seen_values, own, kv_send, kv_got, q_send, q_got, k_pass, k_got, v_pass, v_got, o_send, o_got
):
    heads = lax.axis_size("head")
    seqs, me, plane, member = place()
    base = plane * GROUP
    has_above = plane < groups - 1
    has_below = plane > 0
    barrier = pltpu.get_barrier_semaphore()
    for bits in ORDER:
        greet(barrier, seqs, base + flipped(member, bits))

    @pl.when(has_above)
    def _():
        greet(barrier, seqs, me + GROUP)

    @pl.when(has_below)
    def _():
        greet(barrier, seqs, me - GROUP)

    def narrow(ref, to):
        return ref.at[:, pl.ds(pl.multiple_of(to * HEAD_WIDTH, HEAD_WIDTH), HEAD_WIDTH)]

    def wide(ref, to):
        return ref.at[:, pl.ds(pl.multiple_of(to * WIDE, WIDE), WIDE)]

    def remote(src, dst, send, got, to):
        return pltpu.make_async_remote_copy(
            src_ref=src,
            dst_ref=dst,
            send_sem=send,
            recv_sem=got,
            device_id=(to // seqs, to % seqs),
            device_id_type=MESH,
        )

    stay = [
        pltpu.make_async_copy(narrow(k_in, member), keys.at[me], own.at[0]),
        pltpu.make_async_copy(narrow(v_in, member), values.at[me], own.at[1]),
        pltpu.make_async_copy(wide(q_in, member), queries.at[member], own.at[2]),
    ]
    for copy in stay:
        copy.start()
    pl.semaphore_wait(
        barrier, GROUP - 1 + jnp.where(has_above, 1, 0) + jnp.where(has_below, 1, 0)
    )
    stages = stages_for(seqs)
    each = GROUP // stages

    def near_kv(which, owner, to):
        ref, kept = ((k_in, keys), (v_in, values))[which]
        return remote(
            narrow(ref, to),
            kept.at[base + owner],
            kv_send.at[which, to],
            kv_got.at[which, owner],
            base + to,
        )

    def near_q(owner, to):
        return remote(
            wide(q_in, to), queries.at[owner], q_send.at[to], q_got.at[owner], base + to
        )

    for which in range(2):
        for bits in ORDER:
            near_kv(which, member, flipped(member, bits)).start()
    for bits in ORDER:
        near_q(member, flipped(member, bits)).start()

    def relay(ref, send, got):
        def up(block):
            return remote(ref.at[block], ref.at[block], send.at[0, block], got.at[block], me + GROUP)

        def down(block):
            return remote(ref.at[block], ref.at[block], send.at[1, block], got.at[block], me - GROUP)

        def pass_on(block, upward, downward):
            if upward:

                @pl.when(has_above)
                def _():
                    up(block).start()

            if downward:

                @pl.when(has_below)
                def _():
                    down(block).start()

        def far(step, other):
            lower = (plane - step) * GROUP + other
            upper = (plane + step) * GROUP + other

            @pl.when(plane - step >= 0)
            def _():
                up(lower).wait_recv()
                pass_on(lower, True, False)

            @pl.when(plane + step < groups)
            def _():
                down(upper).wait_recv()
                pass_on(upper, False, True)

        def sent(step, carry):
            for other in range(GROUP):
                block = step * GROUP + other

                @pl.when(has_above & (step <= plane))
                def _():
                    up(block).wait_send()

                @pl.when(has_below & (step >= plane))
                def _():
                    down(block).wait_send()

            return carry

        return pass_on, far, sent

    k_relay = relay(keys, k_pass, k_got)
    v_relay = relay(values, v_pass, v_got)

    def set_off(phase):
        stage, which = phase // 2, phase % 2
        for i in range(each):
            t = stage + stages * i

            @pl.when(member == t)
            def _():
                stay[which].wait()

            @pl.when(member != t)
            def _():
                near_kv(which, t, t).wait_recv()

            (k_relay, v_relay)[which][0](base + t, True, True)

    def note(phase):
        if stages == 1:
            return
        stage, which = phase // 2, phase % 2
        kept, seen = ((keys, seen_keys), (values, seen_values))[which]

        def note_step(n, carry):
            at = (n // each) * GROUP + stage + stages * (n % each)
            seen[at] = kept[at]
            return carry

        lax.fori_loop(0, groups * each, note_step, 0)

    slash_slots = slashes.shape[0]
    column_slots = verticals.shape[0]
    factor = math.log2(math.e) / math.sqrt(HEAD_WIDTH)
    key_blocks, value_blocks = (keys, values) if stages == 1 else (seen_keys, seen_values)
    in_stage = SHARED * each
    steps = (groups - 1) * each

    def holder(block):
        return lax.rem(block, heads) * seqs + lax.div(block, heads)

    def product(left, right, dims):
        return lax.dot_general(left, right, (dims, ((), ())), preferred_element_type=jnp.float32)

    def unit_facts(unit):
        head = member * SHARED + unit // GROUP
        number = base + unit % GROUP
        return head, number, lax.rem(number, seqs) * heads + lax.div(number, seqs)

    def score_unit(unit):
        head, number, block = unit_facts(unit)
        at = pl.multiple_of(unit // GROUP * HEAD_WIDTH, HEAD_WIDTH)
        query = queries[unit % GROUP, :, pl.ds(at, HEAD_WIDTH)]
        rows = lax.broadcasted_iota(jnp.int32, (BLOCK_TOKENS, BLOCK_TOKENS), 0)
        cols = lax.broadcasted_iota(jnp.int32, (BLOCK_TOKENS, BLOCK_TOKENS), 1)
        best = product(query, key_blocks[number], ((1,), (1,)))
        best = jnp.where(rows >= cols, best, -jnp.inf)
        scores[unit, 0] = best
        for slot in range(slash_slots):
            other = block - slashes[slot, head]
            active = (other >= 0) & (slot < counts[1, head])
            found = product(query, key_blocks[holder(jnp.maximum(other, 0))], ((1,), (1,)))
            found = jnp.where(active, found, -jnp.inf)
            scores[unit, 1 + slot] = found
            best = jnp.maximum(best, found)
        for slot in range(column_slots):
            column = verticals[slot, head]
            active = (column < block) & (slot < counts[0, head])
            for s in range(slash_slots):
                repeated = (block - column == slashes[s, head]) & (s < counts[1, head])
                active = active & jnp.logical_not(repeated)
            found = product(query, key_blocks[holder(jnp.minimum(column, block))], ((1,), (1,)))
            found = jnp.where(active, found, -jnp.inf)
            scores[unit, 1 + slash_slots + slot] = found
            best = jnp.maximum(best, found)
        top[unit] = jnp.broadcast_to(jnp.max(best, axis=1, keepdims=True), top.shape[1:])

    def mix_unit(unit):
        head, number, block = unit_facts(unit)
        places = [number]
        for slot in range(slash_slots):
            places.append(holder(jnp.maximum(block - slashes[slot, head], 0)))
        for slot in range(column_slots):
            places.append(holder(jnp.minimum(verticals[slot, head], block)))
        total = mixed = None
        for slot, at in enumerate(places):
            weights = jnp.exp2((scores[unit, slot] - top[unit]) * factor)
            part = product(weights.astype(jnp.bfloat16), value_blocks[at], ((1,), (0,)))
            total = weights if total is None else total + weights
            mixed = part if mixed is None else mixed + part
        mixed = mixed / jnp.sum(total, axis=1, keepdims=True)
        results[unit] = mixed.astype(jnp.bfloat16)

    def unit_in(stage, n):
        return n // each * GROUP + stage + stages * (n % each)

    def column_of(ref, owner, j):
        at = pl.multiple_of((owner * SHARED + j) * HEAD_WIDTH, HEAD_WIDTH)
        return ref.at[:, pl.ds(at, HEAD_WIDTH)]

    def give(j, owner, t):
        return remote(
            results.at[j * GROUP + t],
            column_of(out, owner, j),
            o_send.at[j, t],
            o_got.at[j, owner],
            base + t,
        )

    def hold(j):
        return pltpu.make_async_copy(
            results.at[j * GROUP + member], column_of(out, member, j), own.at[3 + j]
        )

    def hand_out(unit):
        j, t = unit // GROUP, unit % GROUP

        @pl.when(t != member)
        def _():
            give(j, member, t).start()

        @pl.when(t == member)
        def _():
            hold(j).start()

    def q_ready(stage):
        for i in range(each):
            t = stage + stages * i

            @pl.when(member == t)
            def _():
                stay[2].wait()

            @pl.when(member != t)
            def _():
                near_q(t, t).wait_recv()

    def between(far, first, count, total, work, after):
        def piece(n, carry):
            start, stop = n * total // count, (n + 1) * total // count

            def inner(u, carry):
                work(u)
                return carry

            lax.fori_loop(start, stop, inner, 0)
            far(first + n)
            if after is not None:

                def later(u, carry):
                    after(u)
                    return carry

                lax.fori_loop(start, stop, later, 0)
            return carry

        lax.fori_loop(0, count, piece, 0)

    def job_of(kind, stage):
        if kind == 0:
            return in_stage, (lambda u: score_unit(unit_in(stage, u))), None

        def mix(u):
            mix_unit(unit_in(stage, 2 * u))
            mix_unit(unit_in(stage, 2 * u + 1))

        def send(u):
            hand_out(unit_in(stage, 2 * u))
            hand_out(unit_in(stage, 2 * u + 1))

        return in_stage // 2, mix, send

    phases = 2 * stages
    jobs = [(kind, stage) for stage in range(stages) for kind in range(2)]
    opening = min(4, phases - 1)
    for phase in range(min(2, phases)):
        set_off(phase)
    for phase in range(phases):
        stage, which = phase // 2, phase % 2
        if phase + 2 < phases:
            set_off(phase + 2)
        far_step = (k_relay, v_relay)[which][1]

        def far(n, far_step=far_step, stage=stage):
            far_step(n // each + 1, stage + stages * (n % each))

        now = []
        while phase >= opening and len(now) < 2 and jobs and 2 * jobs[0][1] + jobs[0][0] < phase:
            now.append(jobs.pop(0))
        done = 0
        for at, (kind, work_stage) in enumerate(now):
            if kind == 0:
                q_ready(work_stage)
            share = steps * (at + 1) // len(now) - done
            between(far, done, share, *job_of(kind, work_stage))
            done += share
        if not now:
            between(far, 0, steps, 0, lambda u: None, None)
        note(phase)
    for kind, stage in jobs:
        total, work, after = job_of(kind, stage)
        if kind == 0:
            q_ready(stage)

        def last(n, carry, work=work, after=after):
            work(n)
            if after is not None:

                @pl.when(n > 0)
                def _():
                    after(n - 1)

            return carry

        lax.fori_loop(0, total, last, 0)
        if after is not None:
            after(total - 1)
    for bits in ORDER:
        to = flipped(member, bits)
        near_kv(0, member, to).wait_send()
        near_kv(1, member, to).wait_send()
        near_q(member, to).wait_send()
    lax.fori_loop(0, groups, k_relay[2], 0)
    lax.fori_loop(0, groups, v_relay[2], 0)
    for j in range(SHARED):
        hold(j).wait()
        for bits in ORDER:
            other = flipped(member, bits)
            give(j, member, other).wait_send()
            give(j, other, other).wait_recv()


def shards(queries, key_row_matrix, values, verticals, slashes, counts):
    rows, width = queries.shape[1:]
    assert rows == BLOCK_TOKENS
    groups = lax.axis_size("head") * lax.axis_size("seq") // GROUP
    count = groups * GROUP
    units = SHARED * GROUP
    slots = 1 + verticals.shape[1] + slashes.shape[1]
    block = (BLOCK_TOKENS, HEAD_WIDTH)
    seen = count if stages_for(lax.axis_size("seq")) > 1 else 1
    out = pl.pallas_call(
        functools.partial(kernel, groups),
        name="block_sparse_attention",
        out_shape=jax.ShapeDtypeStruct((rows, width), jnp.bfloat16),
        in_specs=[SMEM] * 3 + [ANY] * 3,
        out_specs=ANY,
        scratch_shapes=[
            pltpu.VMEM((GROUP, rows, WIDE), jnp.bfloat16),
            pltpu.VMEM((count,) + block, jnp.bfloat16),
            pltpu.VMEM((count,) + block, jnp.bfloat16),
            pltpu.VMEM((units, slots, BLOCK_TOKENS, BLOCK_TOKENS), jnp.float32),
            pltpu.VMEM((units, BLOCK_TOKENS, BLOCK_TOKENS), jnp.float32),
            pltpu.VMEM((units,) + block, jnp.bfloat16),
            pltpu.VMEM((seen,) + block, jnp.bfloat16),
            pltpu.VMEM((seen,) + block, jnp.bfloat16),
            pltpu.SemaphoreType.DMA((3 + SHARED,)),
            pltpu.SemaphoreType.DMA((2, GROUP)),
            pltpu.SemaphoreType.DMA((2, GROUP)),
            pltpu.SemaphoreType.DMA((GROUP,)),
            pltpu.SemaphoreType.DMA((GROUP,)),
            pltpu.SemaphoreType.DMA((2, count)),
            pltpu.SemaphoreType.DMA((count,)),
            pltpu.SemaphoreType.DMA((2, count)),
            pltpu.SemaphoreType.DMA((count,)),
            pltpu.SemaphoreType.DMA((SHARED, GROUP)),
            pltpu.SemaphoreType.DMA((SHARED, GROUP)),
        ],
        compiler_params=pltpu.CompilerParams(
            collective_id=0, has_side_effects=True, vmem_limit_bytes=VMEM_BYTES
        ),
    )(verticals.T, slashes.T, counts.T, queries[0], key_row_matrix[0], values[0])
    return out[None]


def solution(mesh):
    in_specs = (
        P("seq", "head", None),
        P("seq", "head", None),
        P("seq", "head", None),
        P(),
        P(),
        P(),
    )
    out_specs = P("seq", "head", None)
    return jax.shard_map(shards, mesh=mesh, in_specs=in_specs, out_specs=out_specs, check_vma=False)
```
